1024 devices in a mesh: rows: 64 (over y, x), vecs: 16 (over z, core).
Axes of the slice: x: 8, y: 8, z: 8, core: 2. Of those that a mesh axis runs over, the one named last changes fastest.
Arguments:
- vectors: float32 [8192, 2048], P('rows', 'vecs'), may hold values from -6 to 6
- reflectors: float32 [3, 64, 128, 256], P(None, 'rows', 'vecs'), may hold values from -3 to 3
Outputs:
- transformed: float32 [8192, 2048], P('rows', 'vecs')
The draws below stay inside these ranges and needn't reach their ends.
All inputs are finite; a program needn't handle non-finite values.
Results may differ from the reference program's by a relative error of at most 0.0003.
Values sent between devices are 32-bit elements; how exact they have to be, the bound alone decides.
A program may use at most 32 MiB of HBM per device.

```python
import math
import jax
import jax.numpy as jnp
from jax import lax

KB = 128
GROUPS = 3
NROWS = 8192
NVECS = 2048
NBLK = 64


def draw_reflectors(key, part):
    basis_key = jax.random.fold_in(key, 23)
    noise_key = jax.random.fold_in(key, 11)
    scale_key = jax.random.fold_in(key, 37)
    gaussian = jax.random.normal(basis_key, (GROUPS, NBLK, KB, KB), jnp.float32)
    orthogonal = jnp.linalg.qr(gaussian)[0]
    identity = jnp.broadcast_to(jnp.eye(KB, dtype=jnp.float32), orthogonal.shape)
    pattern = jnp.concatenate([identity, -orthogonal], 3)
    spread = 0.05 / math.sqrt(KB)
    jitter = jnp.clip(jax.random.normal(noise_key, pattern.shape, jnp.float32), -4.0, 4.0) * spread
    log_scale = jax.random.uniform(scale_key, (GROUPS, NBLK, KB, 1), jnp.float32, math.log(0.5), math.log(2.0))
    return jnp.exp(log_scale) * (pattern + jitter)


def levels(key, dims, shards, least, top_value):
    gain, own = 1.0, jax.random.fold_in(key, 6)
    for dim, shards_of in shards:
        draws = jnp.exp(jax.random.uniform(jax.random.fold_in(own, dim), (shards_of,), jnp.float32, least / len(shards), top_value / len(shards)))
        gain = gain * jnp.repeat(draws, dims[dim] // shards_of).reshape([-1 if axis == dim else 1 for axis in range(len(dims))])
    return gain


def normal_values(own_key, shape, deviation, reach, cuts=(), kind=jnp.bfloat16):
    gain = levels(own_key, shape, cuts, -0.22, 0.18) if cuts else 1.0
    values = jax.random.normal(own_key, shape, jnp.float32) * deviation * gain
    return jnp.minimum(jnp.maximum(values, -reach), reach).astype(kind)


def setup_inputs(seed: int = 0) -> dict:
    key_list = jax.random.split(jax.random.key(seed), 3)
    return {
        "vectors": normal_values(key_list[0], (NROWS, NVECS), 1.0, 6.0, ((0, 64), (1, 16)), jnp.float32),
        "reflectors": draw_reflectors(jax.random.fold_in(key_list[2], 71), 0),
    }


HIGHEST = lax.Precision.HIGHEST

def factor(reflector):
    gram_matrix = jnp.dot(reflector, reflector.T, precision=HIGHEST)
    return jnp.triu(gram_matrix, 1) + jnp.diag(jnp.diag(gram_matrix)) * 0.5

def reflect(window_rows, reflector, inv_factor):
    weights = jnp.dot(reflector, window_rows, precision=HIGHEST)
    solved = lax.linalg.triangular_solve(inv_factor, weights, left_side=True, lower=False)
    return window_rows - jnp.dot(reflector.T, solved, precision=HIGHEST)

def reference(vectors, reflectors):
    block_size = reflectors.shape[2]
    block_count = reflectors.shape[1]
    row_pos = lax.broadcasted_iota(jnp.int32, reflectors.shape, 3)
    block_pos = lax.broadcasted_iota(jnp.int32, reflectors.shape, 1)
    masked = jnp.where((block_pos == block_count - 1) & (row_pos >= block_size), jnp.zeros_like(reflectors), reflectors)
    padded = jnp.concatenate([vectors, jnp.zeros((block_size, vectors.shape[1]), vectors.dtype)], 0)
    for group in range(GROUPS):
        group_blocks = masked[group]

        def advance(block, state):
            block_index = jnp.asarray(block).astype(jnp.int32)
            reflector = lax.dynamic_index_in_dim(group_blocks, block_index, 0, keepdims=False)
            start_row = (block_index * block_size).astype(jnp.int32)
            window_rows = lax.dynamic_slice_in_dim(state, start_row, 2 * block_size, 0)
            updated = reflect(window_rows, reflector, factor(reflector))
            return lax.dynamic_update_slice_in_dim(state, updated, start_row, 0)
        padded = lax.fori_loop(0, block_count, advance, padded)
    return padded[:NROWS]
```

```python
import functools

import jax
import jax.numpy as jnp
from jax import lax
from jax.experimental import pallas as pl
from jax.experimental.pallas import tpu as pltpu
from jax.sharding import PartitionSpec as P

HIGHEST = lax.Precision.HIGHEST
MESH = pl.DeviceIdType.MESH
CHUNK = 32


def hdot(a, b):
    return jnp.dot(a, b, precision=HIGHEST, preferred_element_type=jnp.float32)


def split(value):
    high = value.astype(jnp.bfloat16)
    low = (value - high.astype(jnp.float32)).astype(jnp.bfloat16)
    return high, low


def unit_lower_inverse(strict):
    n = strict.shape[0]
    row = lax.broadcasted_iota(jnp.int32, (n, n), 0)
    col = lax.broadcasted_iota(jnp.int32, (n, n), 1)
    result = jnp.where(row == col, 1.0, 0.0).astype(jnp.float32)
    size = 1
    while size < n:
        wide = 2 * size
        pair = (row // wide == col // wide) & (row % wide >= size) & (col % wide < size)
        corner = jnp.where(pair, strict, 0.0)
        if size == 1:
            result = result - corner
        else:
            result = result - hdot(hdot(result, corner), result)
        size = wide
    return result


def block_map(block):
    n = block.shape[0]
    gram = lax.dot_general(block, block, (((1,), (1,)), ((), ())), precision=HIGHEST, preferred_element_type=jnp.float32)
    row = lax.broadcasted_iota(jnp.int32, (n, n), 0)
    col = lax.broadcasted_iota(jnp.int32, (n, n), 1)
    diagonal = jnp.where(row == col, gram * 0.5, 0.0)
    half_row = jnp.sum(diagonal, axis=0, keepdims=True)
    half_col = jnp.sum(diagonal, axis=1, keepdims=True)
    strict = jnp.where(row > col, gram / half_row, 0.0)
    solved = hdot(unit_lower_inverse(strict), block) / half_col
    return hdot(block.T, solved)


def kernel(n_rows, n_vecs, x_ref, refl_ref, out_ref, blocks, maps, lower, carry, done, passed,
           ag_send, ag_recv, low_send, low_recv, car_send, car_recv):
    groups, size = blocks.shape[0], blocks.shape[1]
    cols = x_ref.shape[1]
    n_chunks = cols // CHUNK
    r, v = lax.axis_index("rows"), lax.axis_index("vecs")
    above, below = lax.rem(r + n_rows - 1, n_rows), lax.rem(r + 1, n_rows)
    first, last = r == 0, r == n_rows - 1
    piece = size // n_vecs
    n_chips = n_vecs // 2
    core = lax.rem(v, 2)
    partner = v + 1 - 2 * core
    others = [lax.rem(v + 2 * step, n_vecs) for step in range(1, n_chips)]
    sources = [lax.rem(v - 2 * step + n_vecs, n_vecs) for step in range(1, n_chips)]

    barrier = pltpu.get_barrier_semaphore()
    for peer in [(r, partner)] + [(r, other) for other in others] + [(above, v), (below, v)]:
        pl.semaphore_signal(barrier, inc=1, device_id=peer, device_id_type=MESH)
    pl.semaphore_wait(barrier, n_chips + 2)

    def rows_of(vec):
        return pl.ds(pl.multiple_of(vec * piece, piece), piece)

    sends = []
    for k, peer in enumerate(others + [partner]):
        sends.append(pltpu.make_async_remote_copy(
            refl_ref.at[:, 0], blocks.at[:, rows_of(v)], ag_send.at[k], ag_recv.at[v],
            device_id=(r, peer), device_id_type=MESH))
        sends[-1].start()

    done[0] = x_ref[...].T

    def lower_copy(g, j):
        at = pl.ds(j * CHUNK, CHUNK)
        return pltpu.make_async_remote_copy(
            done.at[g, at], lower.at[g, at], low_send.at[g, j], low_recv.at[g, j],
            device_id=(above, v), device_id_type=MESH)

    def carry_copy(g, j):
        at = pl.ds(j * CHUNK, CHUNK)
        return pltpu.make_async_remote_copy(
            passed.at[g, at], carry.at[g, at], car_send.at[g, j], car_recv.at[g, j],
            device_id=(below, v), device_id_type=MESH)

    @pl.when(jnp.logical_not(first))
    def _():
        for j in range(n_chunks):
            lower_copy(0, j).start()

    @pl.when(first)
    def _():
        carry[0] = done[0]

    @pl.when(last)
    def _():
        lower[...] = jnp.zeros_like(lower)

    blocks[:, rows_of(v)] = refl_ref[:, 0]

    def arrived(vec):
        pltpu.make_async_remote_copy(
            refl_ref.at[:, 0], blocks.at[:, rows_of(vec)], ag_send.at[0], ag_recv.at[vec],
            device_id=(r, partner), device_id_type=MESH).wait_recv()

    order = sorted(range(1, n_chips), key=lambda step: min(step, n_chips - step))
    for step in order:
        source = sources[step - 1]
        arrived(source)
        sends.append(pltpu.make_async_remote_copy(
            blocks.at[:, rows_of(source)], blocks.at[:, rows_of(source)],
            ag_send.at[n_chips + step - 1], ag_recv.at[source],
            device_id=(r, partner), device_id_type=MESH))
        sends[-1].start()
    arrived(partner)
    for step in order:
        arrived(lax.rem(partner - 2 * step + n_vecs, n_vecs))
    for copy in sends:
        copy.wait_send()

    wide = 2 * size
    keep = jnp.logical_not(last) | (lax.broadcasted_iota(jnp.int32, (size, wide), 1) < size)
    for g in range(groups):
        full = block_map(jnp.where(keep, blocks[g], 0.0))
        high, low = split(full)
        for part in range(2):
            at = slice(part * size, (part + 1) * size)
            maps[g, part, 0:size] = high[at]
            maps[g, part, size:2 * size] = high[at]
            maps[g, part, 2 * size:3 * size] = low[at]

    def product(value, g, part):
        high, low = split(value)
        return jnp.dot(jnp.concatenate([high, low, high], axis=1), maps[g, part],
                       preferred_element_type=jnp.float32)

    for g in range(groups):
        for j in range(n_chunks):
            at = slice(j * CHUNK, (j + 1) * CHUNK)

            @pl.when(jnp.logical_not(last))
            def _():
                lower_copy(g, j).wait_recv()

            under = lower[g, at]
            base = product(under, g, 1)

            @pl.when(jnp.logical_not(first))
            def _():
                carry_copy(g, j).wait_recv()

            top = carry[g, at]
            taken = base + product(top, g, 0)
            passed[g, at] = under - taken[:, size:]

            @pl.when(jnp.logical_not(last))
            def _():
                carry_copy(g, j).start()

            final = top - taken[:, :size]
            if g == groups - 1:
                out_ref[at] = final
            else:
                done[g + 1, at] = final

                @pl.when(jnp.logical_not(first))
                def _():
                    lower_copy(g + 1, j).start()

                @pl.when(first)
                def _():
                    carry[g + 1, at] = final

    @pl.when(jnp.logical_not(last))
    def _():
        for g in range(groups):
            for j in range(n_chunks):
                carry_copy(g, j).wait_send()

    @pl.when(jnp.logical_not(first))
    def _():
        for g in range(groups):
            for j in range(n_chunks):
                lower_copy(g, j).wait_send()


def local(n_rows, n_vecs, vectors, reflectors):
    size, cols = vectors.shape
    groups, wide = reflectors.shape[0], reflectors.shape[3]
    n_chunks = cols // CHUNK
    slab = pltpu.VMEM((groups, cols, size), jnp.float32)
    dma = pltpu.SemaphoreType.DMA
    out = pl.pallas_call(
        functools.partial(kernel, n_rows, n_vecs),
        out_shape=jax.ShapeDtypeStruct((cols, size), jnp.float32),
        in_specs=[pl.BlockSpec(memory_space=pltpu.VMEM)] * 2,
        out_specs=pl.BlockSpec(memory_space=pltpu.VMEM),
        scratch_shapes=[
            pltpu.VMEM((groups, size, wide), jnp.float32),
            pltpu.VMEM((groups, 2, 3 * size, wide), jnp.bfloat16),
            slab, slab, slab, slab,
            dma((n_vecs,)), dma((n_vecs,)),
            dma((groups, n_chunks)), dma((groups, n_chunks)),
            dma((groups, n_chunks)), dma((groups, n_chunks)),
        ],
        compiler_params=pltpu.CompilerParams(collective_id=0, has_side_effects=True),
        name="chain",
    )(vectors, reflectors)
    return out.T


def solution(mesh):
    n_rows, n_vecs = mesh.shape["rows"], mesh.shape["vecs"]
    placed = (P("rows", "vecs"), P(None, "rows", "vecs", None))
    return jax.shard_map(
        functools.partial(local, n_rows, n_vecs), mesh=mesh, in_specs=placed,
        out_specs=P("rows", "vecs"), check_vma=False)
```

```python
import functools

import jax
import jax.numpy as jnp
from jax import lax
from jax.experimental import pallas as pl
from jax.experimental.pallas import tpu as pltpu
from jax.sharding import PartitionSpec as P

HIGHEST = lax.Precision.HIGHEST
MESH = pl.DeviceIdType.MESH
ACROSS = 8


def hdot(a, b):
    return jnp.dot(a, b, precision=HIGHEST, preferred_element_type=jnp.float32)


def split(value):
    high = value.astype(jnp.bfloat16)
    low = (value - high.astype(jnp.float32)).astype(jnp.bfloat16)
    return high, low


def inverse_factors(blocks):
    n = blocks[0].shape[0]
    row = lax.broadcasted_iota(jnp.int32, (n, n), 0)
    col = lax.broadcasted_iota(jnp.int32, (n, n), 1)
    stricts, halves = [], []
    for block in blocks:
        gram = lax.dot_general(block, block, (((1,), (1,)), ((), ())), precision=HIGHEST,
                               preferred_element_type=jnp.float32)
        diagonal = jnp.where(row == col, gram * 0.5, 0.0)
        halves.append(jnp.sum(diagonal, axis=1, keepdims=True))
        stricts.append(jnp.where(row > col, gram / jnp.sum(diagonal, axis=0, keepdims=True), 0.0))
    identity = jnp.where(row == col, 1.0, 0.0).astype(jnp.float32)
    results = [identity] * len(blocks)
    size = 1
    while size < n:
        wide = 2 * size
        pair = (row // wide == col // wide) & (row % wide >= size) & (col % wide < size)
        corners = [jnp.where(pair, strict, 0.0) for strict in stricts]
        if size == 1:
            results = [result - corner for result, corner in zip(results, corners)]
        else:
            halfway = [hdot(result, corner) for result, corner in zip(results, corners)]
            results = [result - hdot(half, result) for result, half in zip(results, halfway)]
        size = wide
    return [result / half for result, half in zip(results, halves)]


def kernel(n_rows, n_vecs, nx, x_ref, refl_ref, out_ref, blocks, factors, maps, turned, state, base, carry,
           passed, ready, final, ag_send, ag_recv, in_send, in_recv, ring_send, ring_recv, share_send,
           share_recv, low_send, low_recv, car_send, car_recv, fin_send, fin_recv):
    groups, size, wide = blocks.shape[1:]
    cols = x_ref.shape[1]
    part = cols // nx
    ny = n_rows // nx
    n_chips = n_vecs // 2
    piece = size // n_vecs
    r, v = lax.axis_index("rows"), lax.axis_index("vecs")
    y, x = r // nx, lax.rem(r, nx)
    core = lax.rem(v, 2)
    partner = v + 1 - 2 * core
    first, last = y == 0, y == ny - 1
    inner, outer = jnp.logical_not(first), jnp.logical_not(last)
    above = (lax.rem(r + n_rows - nx, n_rows), v)
    below = (lax.rem(r + nx, n_rows), v)
    mate = (r, partner)
    way = 1 - 2 * core

    def along(step):
        return lax.rem(x + step + 2 * nx, nx)

    def remote(src, dst, sent, got, device):
        return pltpu.make_async_remote_copy(src, dst, sent, got, device_id=device, device_id_type=MESH)

    onward = (y * nx + along(way), v)
    chips = [lax.rem(v + 2 * k, n_vecs) for k in range(1, n_chips)]
    peers = [along(k) for k in range(1, nx)]

    barrier = pltpu.get_barrier_semaphore()
    for device in [mate, above, below] + [(r, c) for c in chips] + [(y * nx + p, v) for p in peers]:
        pl.semaphore_signal(barrier, inc=1, device_id=device, device_id_type=MESH)
    pl.semaphore_wait(barrier, 3 + len(chips) + len(peers))

    def rows_of(vec):
        return pl.ds(pl.multiple_of(vec * piece, piece), piece)

    def cols_of(place):
        return pl.ds(pl.multiple_of(place * part, part), part)

    sends = []
    for k, peer in enumerate(chips + [partner]):
        sends.append(remote(refl_ref.at[:, 0], blocks.at[x, :, rows_of(v)], ag_send.at[k], ag_recv.at[v], (r, peer)))
        sends[-1].start()

    turned[...] = x_ref[...].T
    for k, peer in enumerate(peers):
        sends.append(remote(turned.at[cols_of(peer)], state.at[0, x], in_send.at[k], in_recv.at[x], (y * nx + peer, v)))
        sends[-1].start()
    state[0, x] = turned[cols_of(x)]
    blocks[x, :, rows_of(v)] = refl_ref[:, 0]

    @pl.when(last)
    def _():
        for g in range(groups):
            state[g, nx] = jnp.zeros((part, size), jnp.float32)

    def arrived(vec):
        remote(refl_ref.at[:, 0], blocks.at[x, :, rows_of(vec)], ag_send.at[0], ag_recv.at[vec], mate).wait_recv()

    order = sorted(range(1, n_chips), key=lambda k: min(k, n_chips - k))
    for k in order:
        source = lax.rem(v - 2 * k + n_vecs, n_vecs)
        arrived(source)
        there = blocks.at[x, :, rows_of(source)]
        sends.append(remote(there, there, ag_send.at[n_chips + k - 1], ag_recv.at[source], mate))
        sends[-1].start()
    arrived(partner)
    for k in order:
        arrived(lax.rem(partner - 2 * k + n_vecs, n_vecs))

    far = nx // 2
    stores = (blocks, factors)

    def ring(step, g, kind):
        there = stores[kind].at[along(-way * (step - 1)), g]
        return remote(there, there, ring_send.at[step - 1, g, kind], ring_recv.at[step - 1, g, kind], onward)

    def ring_arrival(step, g, kind):
        there = stores[kind].at[along(-way * step), g]
        return remote(there, there, ring_send.at[step - 1, g, kind], ring_recv.at[step - 1, g, kind], onward)

    def share(step, g, kind, sign):
        there = stores[kind].at[along(-sign * way * step), g]
        return remote(there, there, share_send.at[step - 1, g, kind], share_recv.at[step - 1, g, kind], mate)

    def owner(step, g, kind):
        if step < far:
            return None
        return 0 if g == 0 or (g == 1 and kind == 0) else 1

    def on(core_index, action):
        if core_index is None:
            action()
        else:
            pl.when(core == core_index)(action)

    for g in range(groups):
        on(owner(1, g, 0), lambda: ring(1, g, 0).start())

    for k in range(1, nx):
        source = along(-k)
        remote(turned.at[cols_of(x)], state.at[0, source], in_send.at[0], in_recv.at[source], onward).wait_recv()

    def low(g):
        return remote(state.at[g, 0], state.at[g, nx], low_send.at[g], low_recv.at[g], above)

    @pl.when(inner)
    def _():
        low(0).start()

    lane = lax.broadcasted_iota(jnp.int32, (size, wide), 1)

    def masked(place, g):
        return jnp.where((y * nx + place < n_rows - 1) | (lane < size), blocks[place, g], 0.0)

    for g, inverse in enumerate(inverse_factors([masked(x, g) for g in range(groups)])):
        factors[x, g] = inverse
        on(owner(1, g, 1), lambda: ring(1, g, 1).start())

    def form(place):
        def one(g, nothing):
            block = masked(place, g)
            full = hdot(block.T, hdot(factors[place, g], block))
            maps[place, g, 0], maps[place, g, 1] = split(full)
            return nothing

        lax.fori_loop(0, groups, one, 0)

    form(x)
    for step in range(1, far + 1):
        for kind in range(2):
            for g in range(groups):
                def take():
                    ring_arrival(step, g, kind).wait_recv()
                    if step < far:
                        on(owner(step + 1, g, kind), lambda: ring(step + 1, g, kind).start())
                    share(step, g, kind, 1).start()

                on(owner(step, g, kind), take)
        if step < far:
            form(along(-way * step))
        for kind in range(2):
            for g in range(groups):
                whose = owner(step, g, kind)
                on(None if whose is None else 1 - whose, lambda: share(step, g, kind, -1).wait_recv())
        form(along(way * step))

    def product(value, place, g, half):
        at = slice(half * size, (half + 1) * size)
        high, lower = split(value)
        both = jnp.dot(jnp.concatenate([high, lower], axis=0), maps[place, g, 0, at], preferred_element_type=jnp.float32)
        cross = jnp.dot(high, maps[place, g, 1, at], preferred_element_type=jnp.float32)
        return both[:part] + (both[part:] + cross)

    def pass_on(g):
        return remote(passed.at[g], carry.at[g], car_send.at[g], car_recv.at[g], below)

    def deliver(place, slot):
        return remote(ready.at[slot], final.at[cols_of(x)], fin_send.at[slot], fin_recv.at[x], (y * nx + place, v))

    def prepare(g, place):
        under = state[g, place + 1]
        taken = product(under, place, g, 1)
        base[place, :, :size] = -taken[:, :size]
        base[place, :, size:] = under - taken[:, size:]

    for g in range(groups):
        for place in range(nx - 1):
            prepare(g, place)

        @pl.when(first)
        def _():
            carry[g] = state[g, 0]

        @pl.when(inner)
        def _():
            pass_carry = pass_on(g)
            pass_carry.wait_recv()

        top = carry[g]
        for place in range(nx):
            if place == nx - 1:
                @pl.when(outer)
                def _():
                    low(g).wait_recv()

                prepare(g, place)
            result = base[place] - product(top, place, g, 0)
            done = top + result[:, :size]
            top = result[:, size:]
            if g < groups - 1:
                state[g + 1, place] = done
                if place == 0:
                    @pl.when(inner)
                    def _():
                        low(g + 1).start()
            else:
                ready[place] = done

                @pl.when(x != place)
                def _():
                    deliver(place, place).start()
        passed[g] = top

        @pl.when(outer)
        def _():
            pass_on(g).start()

    final[cols_of(x)] = ready[x]
    for k in range(1, nx):
        source = along(-k)
        remote(ready.at[0], final.at[cols_of(source)], fin_send.at[0], fin_recv.at[source], onward).wait_recv()
    out_ref[...] = final[...]

    for copy in sends:
        copy.wait_send()
    for step in range(1, far + 1):
        for kind in range(2):
            for g in range(groups):
                def finish():
                    ring(step, g, kind).wait_send()
                    share(step, g, kind, 1).wait_send()

                on(owner(step, g, kind), finish)
    for place in range(nx):
        @pl.when(x != place)
        def _():
            deliver(place, place).wait_send()

    @pl.when(outer)
    def _():
        for g in range(groups):
            pass_on(g).wait_send()

    @pl.when(inner)
    def _():
        for g in range(groups):
            low(g).wait_send()


def local(n_rows, n_vecs, nx, vectors, reflectors):
    size, cols = vectors.shape
    groups, wide = reflectors.shape[0], reflectors.shape[3]
    part, far, f32, vmem = cols // nx, nx // 2, jnp.float32, pltpu.VMEM
    dma = pltpu.SemaphoreType.DMA
    out = pl.pallas_call(
        functools.partial(kernel, n_rows, n_vecs, nx),
        out_shape=jax.ShapeDtypeStruct((cols, size), f32),
        in_specs=[pl.BlockSpec(memory_space=vmem)] * 2,
        out_specs=pl.BlockSpec(memory_space=vmem),
        scratch_shapes=[
            vmem((nx, groups, size, wide), f32),
            vmem((nx, groups, size, size), f32),
            vmem((nx, groups, 2, wide, wide), jnp.bfloat16),
            vmem((cols, size), f32),
            vmem((groups, nx + 1, part, size), f32),
            vmem((nx, part, wide), f32),
            vmem((groups, part, size), f32),
            vmem((groups, part, size), f32),
            vmem((nx, part, size), f32),
            vmem((cols, size), f32),
            dma((n_vecs,)), dma((n_vecs,)), dma((nx,)), dma((nx,)),
            dma((far, groups, 2)), dma((far, groups, 2)), dma((far, groups, 2)), dma((far, groups, 2)),
            dma((groups,)), dma((groups,)), dma((groups,)), dma((groups,)), dma((nx,)), dma((nx,)),
        ],
        compiler_params=pltpu.CompilerParams(collective_id=0, has_side_effects=True),
        name="rows",
    )(vectors, reflectors)
    return out.T


def solution(mesh):
    n_rows, n_vecs = mesh.shape["rows"], mesh.shape["vecs"]
    placed = (P("rows", "vecs"), P(None, "rows", "vecs", None))
    return jax.shard_map(
        functools.partial(local, n_rows, n_vecs, ACROSS), mesh=mesh, in_specs=placed,
        out_specs=P("rows", "vecs"), check_vma=False)
```

```python
import functools

import jax
import jax.numpy as jnp
from jax import lax
from jax.experimental import pallas as pl
from jax.experimental.pallas import tpu as pltpu
from jax.sharding import PartitionSpec as P

HIGHEST = lax.Precision.HIGHEST
MESH = pl.DeviceIdType.MESH
ACROSS = 8


def hdot(a, b):
    return jnp.dot(a, b, precision=HIGHEST, preferred_element_type=jnp.float32)


def split(value):
    high = value.astype(jnp.bfloat16)
    low = (value - high.astype(jnp.float32)).astype(jnp.bfloat16)
    return high, low


def product3(left, right):
    (left_high, left_low), (right_high, right_low) = split(left), split(right)

    def dot(a, b):
        return jnp.dot(a, b, preferred_element_type=jnp.float32)

    return dot(left_high, right_high) + (dot(left_low, right_high) + dot(left_high, right_low))


def inverse_factors(blocks):
    n = blocks[0].shape[0]
    row = lax.broadcasted_iota(jnp.int32, (n, n), 0)
    col = lax.broadcasted_iota(jnp.int32, (n, n), 1)
    stricts, halves = [], []
    for block in blocks:
        gram = lax.dot_general(block, block, (((1,), (1,)), ((), ())), precision=HIGHEST,
                               preferred_element_type=jnp.float32)
        diagonal = jnp.where(row == col, gram * 0.5, 0.0)
        halves.append(jnp.sum(diagonal, axis=1, keepdims=True))
        stricts.append(jnp.where(row > col, gram / jnp.sum(diagonal, axis=0, keepdims=True), 0.0))
    identity = jnp.where(row == col, 1.0, 0.0).astype(jnp.float32)
    results = [identity] * len(blocks)
    size = 1
    while size < n:
        wide = 2 * size
        pair = (row // wide == col // wide) & (row % wide >= size) & (col % wide < size)
        corners = [jnp.where(pair, strict, 0.0) for strict in stricts]
        if size == 1:
            results = [result - corner for result, corner in zip(results, corners)]
        else:
            halfway = [hdot(result, corner) for result, corner in zip(results, corners)]
            results = [result - hdot(half, result) for result, half in zip(results, halfway)]
        size = wide
    return [result / half for result, half in zip(results, halves)]


def kernel(n_rows, n_vecs, nx, x_ref, refl_ref, out_ref, blocks, factors, maps, turned, state, base, skip, carry,
           passed, ready, final, ag_send, ag_recv, in_send, in_recv, ring_send, ring_recv, share_send,
           share_recv, low_send, low_recv, car_send, car_recv, fin_send, fin_recv):
    groups, size, wide = blocks.shape[1:]
    cols = x_ref.shape[1]
    part = cols // nx
    ny = n_rows // nx
    n_chips = n_vecs // 2
    piece = size // n_vecs
    r, v = lax.axis_index("rows"), lax.axis_index("vecs")
    y, x = r // nx, lax.rem(r, nx)
    core = lax.rem(v, 2)
    partner = v + 1 - 2 * core
    first, last = y == 0, y == ny - 1
    inner, outer = jnp.logical_not(first), jnp.logical_not(last)
    above = (lax.rem(r + n_rows - nx, n_rows), v)
    below = (lax.rem(r + nx, n_rows), v)
    mate = (r, partner)
    way = 1 - 2 * core

    def along(step):
        return lax.rem(x + step + 2 * nx, nx)

    def remote(src, dst, sent, got, device):
        return pltpu.make_async_remote_copy(src, dst, sent, got, device_id=device, device_id_type=MESH)

    onward = (y * nx + along(way), v)
    chips = [lax.rem(v + 2 * k, n_vecs) for k in range(1, n_chips)]
    peers = [along(k) for k in range(1, nx)]

    barrier = pltpu.get_barrier_semaphore()
    for device in [mate, above, below] + [(r, c) for c in chips] + [(y * nx + p, v) for p in peers]:
        pl.semaphore_signal(barrier, inc=1, device_id=device, device_id_type=MESH)
    pl.semaphore_wait(barrier, 3 + len(chips) + len(peers))

    def rows_of(vec):
        return pl.ds(pl.multiple_of(vec * piece, piece), piece)

    def cols_of(place):
        return pl.ds(pl.multiple_of(place * part, part), part)

    sends = []
    for k, peer in enumerate(chips + [partner]):
        sends.append(remote(refl_ref.at[:, 0], blocks.at[x, :, rows_of(v)], ag_send.at[k], ag_recv.at[v], (r, peer)))
        sends[-1].start()

    turned[...] = x_ref[...].T
    for k, peer in enumerate(peers):
        sends.append(remote(turned.at[cols_of(peer)], state.at[0, x], in_send.at[k], in_recv.at[x], (y * nx + peer, v)))
        sends[-1].start()
    state[0, x] = turned[cols_of(x)]
    blocks[x, :, rows_of(v)] = refl_ref[:, 0]

    @pl.when(last)
    def _():
        for g in range(groups):
            state[g, nx] = jnp.zeros((part, size), jnp.float32)

    def arrived(vec):
        remote(refl_ref.at[:, 0], blocks.at[x, :, rows_of(vec)], ag_send.at[0], ag_recv.at[vec], mate).wait_recv()

    order = sorted(range(1, n_chips), key=lambda k: min(k, n_chips - k))
    for k in order:
        source = lax.rem(v - 2 * k + n_vecs, n_vecs)
        arrived(source)
        there = blocks.at[x, :, rows_of(source)]
        sends.append(remote(there, there, ag_send.at[n_chips + k - 1], ag_recv.at[source], mate))
        sends[-1].start()
    arrived(partner)
    for k in order:
        arrived(lax.rem(partner - 2 * k + n_vecs, n_vecs))

    far = nx // 2
    stores = (blocks, factors)

    def ring(step, g, kind):
        there = stores[kind].at[along(-way * (step - 1)), g]
        return remote(there, there, ring_send.at[step - 1, g, kind], ring_recv.at[step - 1, g, kind], onward)

    def ring_arrival(step, g, kind):
        there = stores[kind].at[along(-way * step), g]
        return remote(there, there, ring_send.at[step - 1, g, kind], ring_recv.at[step - 1, g, kind], onward)

    def share(step, g, kind, sign):
        there = stores[kind].at[along(-sign * way * step), g]
        return remote(there, there, share_send.at[step - 1, g, kind], share_recv.at[step - 1, g, kind], mate)

    def owner(step, kind):
        return None if step < far else kind

    def on(core_index, action):
        if core_index is None:
            action()
        else:
            pl.when(core == core_index)(action)

    def launch(g, kind):
        on(owner(1, kind), lambda: ring(1, g, kind).start())

    launch(0, 0)

    for k in range(1, nx):
        source = along(-k)
        remote(turned.at[cols_of(x)], state.at[0, source], in_send.at[0], in_recv.at[source], onward).wait_recv()

    def low(g):
        return remote(state.at[g, 0], state.at[g, nx], low_send.at[g], low_recv.at[g], above)

    @pl.when(inner)
    def _():
        low(0).start()

    lane = lax.broadcasted_iota(jnp.int32, (size, wide), 1)

    def masked(place, g):
        return jnp.where((y * nx + place < n_rows - 1) | (lane < size), blocks[place, g], 0.0)

    for g, inverse in enumerate(inverse_factors([masked(x, g) for g in range(groups)])):
        factors[x, g] = inverse
        if g == 0:
            launch(0, 1)

    def form(place, g):
        block = masked(place, g)
        full = product3(block.T, product3(factors[place, g], block))
        maps[place, g, 0], maps[place, g, 1] = split(full)

    def spread(g):
        form(x, g)
        for step in range(1, far + 1):
            for kind in range(2):
                def take():
                    ring_arrival(step, g, kind).wait_recv()
                    if step < far:
                        on(owner(step + 1, kind), lambda: ring(step + 1, g, kind).start())
                    share(step, g, kind, 1).start()

                on(owner(step, kind), take)
            if step == max(far - 1, 1) and g < groups - 1:
                launch(g + 1, 0)
                launch(g + 1, 1)
            if step < far:
                form(along(-way * step), g)
            for kind in range(2):
                whose = owner(step, kind)
                on(None if whose is None else 1 - whose, lambda: share(step, g, kind, -1).wait_recv())
            form(along(way * step), g)

    def product(value, place, g, half):
        at = slice(half * size, (half + 1) * size)
        high, lower = split(value)
        both = jnp.dot(jnp.concatenate([high, lower], axis=0), maps[place, g, 0, at], preferred_element_type=jnp.float32)
        cross = jnp.dot(high, maps[place, g, 1, at], preferred_element_type=jnp.float32)
        return both[:part] + (both[part:] + cross)

    def pass_on(g):
        return remote(passed.at[g], carry.at[g], car_send.at[g], car_recv.at[g], below)

    def deliver(place, slot):
        return remote(ready.at[slot], final.at[cols_of(x)], fin_send.at[slot], fin_recv.at[x], (y * nx + place, v))

    def prepare(g, place):
        under = state[g, place + 1]
        taken = product(under, place, g, 1)
        base[place, :, :size] = -taken[:, :size]
        base[place, :, size:] = under - taken[:, size:]

    def send_carry(g):
        @pl.when(outer)
        def _():
            pass_on(g).start()

    def begin(g, at_first):
        for place in range(nx - 1):
            prepare(g, place)
        if at_first:
            return
        right = slice(size, wide)
        start = maps[0, g, 0, :size, right].astype(jnp.float32) + maps[0, g, 1, :size, right].astype(jnp.float32)
        through = jnp.concatenate([-start, base[0, :, right]], axis=0)
        rows = size + part
        for place in range(1, nx):
            high, lower = split(through)
            both = jnp.dot(jnp.concatenate([high, lower], axis=0), maps[place, g, 0, :size, right],
                           preferred_element_type=jnp.float32)
            cross = jnp.dot(high, maps[place, g, 1, :size, right], preferred_element_type=jnp.float32)
            through = -(both[:rows] + (both[rows:] + cross))
            if place < nx - 1:
                through = jnp.concatenate([through[:size], through[size:] + base[place, :, right]], axis=0)
        skip[g] = through

    def chain(g, at_first):
        if g > 0:
            begin(g, at_first)

        @pl.when(outer)
        def _():
            low(g).wait_recv()

        prepare(g, nx - 1)
        if at_first:
            top = state[g, 0]
        else:
            pass_on(g).wait_recv()
            top = carry[g]
            passed[g] = product3(top, skip[g, :size]) + (skip[g, size:] + base[nx - 1, :, size:])
            send_carry(g)
        for place in range(nx):
            result = base[place] - product(top, place, g, 0)
            done = top + result[:, :size]
            top = result[:, size:]
            if g < groups - 1:
                state[g + 1, place] = done
                if place == 0 and not at_first:
                    low(g + 1).start()
            else:
                ready[place] = done

                @pl.when(x != place)
                def _():
                    deliver(place, place).start()
        if at_first:
            passed[g] = top
            send_carry(g)

    def chain_where(condition, g, at_first):
        @pl.when(condition)
        def _():
            chain(g, at_first)

    early = inner & (y <= 2)
    spread(0)

    @pl.when(first)
    def _():
        begin(0, True)
        chain(0, True)

    @pl.when(inner)
    def _():
        begin(0, False)

    spread(1)
    chain_where(first, 1, True)
    chain_where(early, 0, False)
    spread(2)
    chain_where(y > 2, 0, False)
    chain_where(inner, 1, False)
    chain_where(first, 2, True)
    chain_where(inner, 2, False)

    final[cols_of(x)] = ready[x]
    for k in range(1, nx):
        source = along(-k)
        remote(ready.at[0], final.at[cols_of(source)], fin_send.at[0], fin_recv.at[source], onward).wait_recv()
    out_ref[...] = final[...]

    for copy in sends:
        copy.wait_send()
    for step in range(1, far + 1):
        for kind in range(2):
            for g in range(groups):
                def finish():
                    ring(step, g, kind).wait_send()
                    share(step, g, kind, 1).wait_send()

                on(owner(step, kind), finish)
    for place in range(nx):
        @pl.when(x != place)
        def _():
            deliver(place, place).wait_send()

    @pl.when(outer)
    def _():
        for g in range(groups):
            pass_on(g).wait_send()

    @pl.when(inner)
    def _():
        for g in range(groups):
            low(g).wait_send()


def local(n_rows, n_vecs, nx, vectors, reflectors):
    size, cols = vectors.shape
    groups, wide = reflectors.shape[0], reflectors.shape[3]
    part, far, f32, vmem = cols // nx, nx // 2, jnp.float32, pltpu.VMEM
    dma = pltpu.SemaphoreType.DMA
    out = pl.pallas_call(
        functools.partial(kernel, n_rows, n_vecs, nx),
        out_shape=jax.ShapeDtypeStruct((cols, size), f32),
        in_specs=[pl.BlockSpec(memory_space=vmem)] * 2,
        out_specs=pl.BlockSpec(memory_space=vmem),
        scratch_shapes=[
            vmem((nx, groups, size, wide), f32),
            vmem((nx, groups, size, size), f32),
            vmem((nx, groups, 2, wide, wide), jnp.bfloat16),
            vmem((cols, size), f32),
            vmem((groups, nx + 1, part, size), f32),
            vmem((nx, part, wide), f32),
            vmem((groups, size + part, size), f32),
            vmem((groups, part, size), f32),
            vmem((groups, part, size), f32),
            vmem((nx, part, size), f32),
            vmem((cols, size), f32),
            dma((n_vecs,)), dma((n_vecs,)), dma((nx,)), dma((nx,)),
            dma((far, groups, 2)), dma((far, groups, 2)), dma((far, groups, 2)), dma((far, groups, 2)),
            dma((groups,)), dma((groups,)), dma((groups,)), dma((groups,)), dma((nx,)), dma((nx,)),
        ],
        compiler_params=pltpu.CompilerParams(collective_id=0, has_side_effects=True),
        name="rows",
    )(vectors, reflectors)
    return out.T


def solution(mesh):
    n_rows, n_vecs = mesh.shape["rows"], mesh.shape["vecs"]
    placed = (P("rows", "vecs"), P(None, "rows", "vecs", None))
    return jax.shard_map(
        functools.partial(local, n_rows, n_vecs, ACROSS), mesh=mesh, in_specs=placed,
        out_specs=P("rows", "vecs"), check_vma=False)
```

```python
import functools

import jax
import jax.numpy as jnp
from jax import lax
from jax.experimental import pallas as pl
from jax.experimental.pallas import tpu as pltpu
from jax.sharding import PartitionSpec as P

HIGHEST = lax.Precision.HIGHEST
MESH = pl.DeviceIdType.MESH
ACROSS = 8


def hdot(a, b):
    return jnp.dot(a, b, precision=HIGHEST, preferred_element_type=jnp.float32)


def split(value):
    high = value.astype(jnp.bfloat16)
    low = (value - high.astype(jnp.float32)).astype(jnp.bfloat16)
    return high, low


def product3(left, right):
    (left_high, left_low), (right_high, right_low) = split(left), split(right)

    def dot(a, b):
        return jnp.dot(a, b, preferred_element_type=jnp.float32)

    return dot(left_high, right_high) + (dot(left_low, right_high) + dot(left_high, right_low))


def inverse_factors(blocks):
    n = blocks[0].shape[0]
    row = lax.broadcasted_iota(jnp.int32, (n, n), 0)
    col = lax.broadcasted_iota(jnp.int32, (n, n), 1)
    stricts, halves = [], []
    for block in blocks:
        gram = lax.dot_general(block, block, (((1,), (1,)), ((), ())), precision=HIGHEST,
                               preferred_element_type=jnp.float32)
        diagonal = jnp.where(row == col, gram * 0.5, 0.0)
        halves.append(jnp.sum(diagonal, axis=1, keepdims=True))
        stricts.append(jnp.where(row > col, gram / jnp.sum(diagonal, axis=0, keepdims=True), 0.0))
    identity = jnp.where(row == col, 1.0, 0.0).astype(jnp.float32)
    results = [identity] * len(blocks)
    size = 1
    while size < n:
        wide = 2 * size
        pair = (row // wide == col // wide) & (row % wide >= size) & (col % wide < size)
        corners = [jnp.where(pair, strict, 0.0) for strict in stricts]
        if size == 1:
            results = [result - corner for result, corner in zip(results, corners)]
        else:
            halfway = [hdot(result, corner) for result, corner in zip(results, corners)]
            results = [result - hdot(half, result) for result, half in zip(results, halfway)]
        size = wide
    return [result / half for result, half in zip(results, halves)]


def kernel(n_rows, n_vecs, nx, x_ref, refl_ref, out_ref, blocks, factors, maps, turned, state, base, skip, carry,
           passed, ready, final, ag_send, ag_recv, in_send, in_recv, ring_send, ring_recv, share_send,
           share_recv, low_send, low_recv, car_send, car_recv, fin_send, fin_recv):
    groups, size, wide = blocks.shape[1:]
    cols = x_ref.shape[1]
    part = cols // nx
    ny = n_rows // nx
    n_chips = n_vecs // 2
    piece = size // n_vecs
    r, v = lax.axis_index("rows"), lax.axis_index("vecs")
    y, x = r // nx, lax.rem(r, nx)
    core = lax.rem(v, 2)
    partner = v + 1 - 2 * core
    first, last = y == 0, y == ny - 1
    inner, outer = jnp.logical_not(first), jnp.logical_not(last)
    above = (lax.rem(r + n_rows - nx, n_rows), v)
    below = (lax.rem(r + nx, n_rows), v)
    mate = (r, partner)
    way = 1 - 2 * core

    def along(step):
        return lax.rem(x + step + 2 * nx, nx)

    def remote(src, dst, sent, got, device):
        return pltpu.make_async_remote_copy(src, dst, sent, got, device_id=device, device_id_type=MESH)

    onward = (y * nx + along(way), v)
    chips = [lax.rem(v + 2 * k, n_vecs) for k in range(1, n_chips)]
    peers = [along(k) for k in range(1, nx)]

    barrier = pltpu.get_barrier_semaphore()
    for device in [mate, above, below] + [(r, c) for c in chips] + [(y * nx + p, v) for p in peers]:
        pl.semaphore_signal(barrier, inc=1, device_id=device, device_id_type=MESH)
    pl.semaphore_wait(barrier, 3 + len(chips) + len(peers))

    def rows_of(vec):
        return pl.ds(pl.multiple_of(vec * piece, piece), piece)

    def cols_of(place):
        return pl.ds(pl.multiple_of(place * part, part), part)

    sends = []
    for k, peer in enumerate(chips + [partner]):
        sends.append(remote(refl_ref.at[:, 0], blocks.at[x, :, rows_of(v)], ag_send.at[k], ag_recv.at[v], (r, peer)))
        sends[-1].start()

    turned[...] = x_ref[...].T
    for k, peer in enumerate(peers):
        sends.append(remote(turned.at[cols_of(peer)], state.at[0, x], in_send.at[k], in_recv.at[x], (y * nx + peer, v)))
        sends[-1].start()
    state[0, x] = turned[cols_of(x)]
    blocks[x, :, rows_of(v)] = refl_ref[:, 0]

    @pl.when(last)
    def _():
        for g in range(groups):
            state[g, nx] = jnp.zeros((part, size), jnp.float32)

    def arrived(vec):
        remote(refl_ref.at[:, 0], blocks.at[x, :, rows_of(vec)], ag_send.at[0], ag_recv.at[vec], mate).wait_recv()

    order = sorted(range(1, n_chips), key=lambda k: min(k, n_chips - k))
    for k in order:
        source = lax.rem(v - 2 * k + n_vecs, n_vecs)
        arrived(source)
        there = blocks.at[x, :, rows_of(source)]
        sends.append(remote(there, there, ag_send.at[n_chips + k - 1], ag_recv.at[source], mate))
        sends[-1].start()
    arrived(partner)
    for k in order:
        arrived(lax.rem(partner - 2 * k + n_vecs, n_vecs))

    far = nx // 2
    stores = (blocks, factors)

    def ring(step, g, kind):
        there = stores[kind].at[along(-way * (step - 1)), g]
        return remote(there, there, ring_send.at[step - 1, g, kind], ring_recv.at[step - 1, g, kind], onward)

    def ring_arrival(step, g, kind):
        there = stores[kind].at[along(-way * step), g]
        return remote(there, there, ring_send.at[step - 1, g, kind], ring_recv.at[step - 1, g, kind], onward)

    def share(step, g, kind, sign):
        there = stores[kind].at[along(-sign * way * step), g]
        return remote(there, there, share_send.at[step - 1, g, kind], share_recv.at[step - 1, g, kind], mate)

    def owner(step, kind):
        return None if step < far else kind

    def on(core_index, action):
        if core_index is None:
            action()
        else:
            pl.when(core == core_index)(action)

    def launch(g, kind):
        on(owner(1, kind), lambda: ring(1, g, kind).start())

    launch(0, 0)

    for k in range(1, nx):
        source = along(-k)
        remote(turned.at[cols_of(x)], state.at[0, source], in_send.at[0], in_recv.at[source], onward).wait_recv()

    def low(g):
        return remote(state.at[g, 0], state.at[g, nx], low_send.at[g], low_recv.at[g], above)

    @pl.when(inner)
    def _():
        low(0).start()

    lane = lax.broadcasted_iota(jnp.int32, (size, wide), 1)

    def masked(place, g):
        return jnp.where((y * nx + place < n_rows - 1) | (lane < size), blocks[place, g], 0.0)

    def factor(*own):
        for g, inverse in zip(own, inverse_factors([masked(x, g) for g in own])):
            factors[x, g] = inverse

    def form(place, g):
        block = masked(place, g)
        full = product3(block.T, product3(factors[place, g], block))
        maps[place, g, 0], maps[place, g, 1] = split(full)

    def spread(slot):
        here = [(slot - g, g) for g in range(groups) if 1 <= slot - g <= far]
        for step, g in here:
            for kind in range(2):
                def take():
                    ring_arrival(step, g, kind).wait_recv()
                    if step < far:
                        on(owner(step + 1, kind), lambda: ring(step + 1, g, kind).start())
                    share(step, g, kind, 1).start()

                on(owner(step, kind), take)
        if slot < groups:
            launch(slot, 0)
            if slot == 1:
                factor(*range(1, groups))
            launch(slot, 1)
            form(x, slot)
        for step, g in here:
            if step < far:
                form(along(-way * step), g)
            for kind in range(2):
                whose = owner(step, kind)
                on(None if whose is None else 1 - whose, lambda: share(step, g, kind, -1).wait_recv())
            form(along(way * step), g)

    factor(0)
    launch(0, 1)
    form(x, 0)

    def product(value, place, g, half):
        at = slice(half * size, (half + 1) * size)
        high, lower = split(value)
        both = jnp.dot(jnp.concatenate([high, lower], axis=0), maps[place, g, 0, at], preferred_element_type=jnp.float32)
        cross = jnp.dot(high, maps[place, g, 1, at], preferred_element_type=jnp.float32)
        return both[:part] + (both[part:] + cross)

    def pass_on(g):
        return remote(passed.at[g], carry.at[g], car_send.at[g], car_recv.at[g], below)

    def deliver(place, slot):
        return remote(ready.at[slot], final.at[cols_of(x)], fin_send.at[slot], fin_recv.at[x], (y * nx + place, v))

    def prepare(g, place):
        under = state[g, place + 1]
        taken = product(under, place, g, 1)
        base[place, :, :size] = -taken[:, :size]
        base[place, :, size:] = under - taken[:, size:]

    def send_carry(g):
        @pl.when(outer)
        def _():
            pass_on(g).start()

    def begin(g, at_first):
        for place in range(nx - 1):
            prepare(g, place)
        if at_first:
            return
        right = slice(size, wide)
        start = maps[0, g, 0, :size, right].astype(jnp.float32) + maps[0, g, 1, :size, right].astype(jnp.float32)
        through = jnp.concatenate([-start, base[0, :, right]], axis=0)
        rows = size + part
        for place in range(1, nx):
            high, lower = split(through)
            both = jnp.dot(jnp.concatenate([high, lower], axis=0), maps[place, g, 0, :size, right],
                           preferred_element_type=jnp.float32)
            cross = jnp.dot(high, maps[place, g, 1, :size, right], preferred_element_type=jnp.float32)
            through = -(both[:rows] + (both[rows:] + cross))
            if place < nx - 1:
                through = jnp.concatenate([through[:size], through[size:] + base[place, :, right]], axis=0)
        skip[g] = through

    def chain(g, at_first):
        @pl.when(outer)
        def _():
            low(g).wait_recv()

        prepare(g, nx - 1)
        if at_first:
            top = state[g, 0]
        else:
            pass_on(g).wait_recv()
            top = carry[g]
            passed[g] = product3(top, skip[g, :size]) + (skip[g, size:] + base[nx - 1, :, size:])
            send_carry(g)
        for place in range(nx):
            result = base[place] - product(top, place, g, 0)
            done = top + result[:, :size]
            top = result[:, size:]
            if g < groups - 1:
                state[g + 1, place] = done
                if place == 0 and not at_first:
                    low(g + 1).start()
            else:
                ready[place] = done

                @pl.when(x != place)
                def _():
                    deliver(place, place).start()
        if at_first:
            passed[g] = top
            send_carry(g)

    early = inner & (y <= 2)
    for slot in range(1, far + 1):
        spread(slot)

    @pl.when(first)
    def _():
        begin(0, True)
        chain(0, True)

    @pl.when(inner)
    def _():
        begin(0, False)

    spread(far + 1)

    @pl.when(first)
    def _():
        begin(1, True)

    @pl.when(early)
    def _():
        chain(0, False)
        begin(1, False)

    for slot in range(far + 2, far + groups):
        spread(slot)

    @pl.when(y > 2)
    def _():
        chain(0, False)
        begin(1, False)

    for at_first, condition in ((True, first), (False, inner)):
        @pl.when(condition)
        def _():
            for g in range(1, groups):
                if g > 1:
                    begin(g, at_first)
                chain(g, at_first)

    final[cols_of(x)] = ready[x]
    for k in range(1, nx):
        source = along(-k)
        remote(ready.at[0], final.at[cols_of(source)], fin_send.at[0], fin_recv.at[source], onward).wait_recv()
    out_ref[...] = final[...]

    for copy in sends:
        copy.wait_send()
    for step in range(1, far + 1):
        for kind in range(2):
            for g in range(groups):
                def finish():
                    ring(step, g, kind).wait_send()
                    share(step, g, kind, 1).wait_send()

                on(owner(step, kind), finish)
    for place in range(nx):
        @pl.when(x != place)
        def _():
            deliver(place, place).wait_send()

    @pl.when(outer)
    def _():
        for g in range(groups):
            pass_on(g).wait_send()

    @pl.when(inner)
    def _():
        for g in range(groups):
            low(g).wait_send()


def local(n_rows, n_vecs, nx, vectors, reflectors):
    size, cols = vectors.shape
    groups, wide = reflectors.shape[0], reflectors.shape[3]
    part, far, f32, vmem = cols // nx, nx // 2, jnp.float32, pltpu.VMEM
    dma = pltpu.SemaphoreType.DMA
    out = pl.pallas_call(
        functools.partial(kernel, n_rows, n_vecs, nx),
        out_shape=jax.ShapeDtypeStruct((cols, size), f32),
        in_specs=[pl.BlockSpec(memory_space=vmem)] * 2,
        out_specs=pl.BlockSpec(memory_space=vmem),
        scratch_shapes=[
            vmem((nx, groups, size, wide), f32),
            vmem((nx, groups, size, size), f32),
            vmem((nx, groups, 2, wide, wide), jnp.bfloat16),
            vmem((cols, size), f32),
            vmem((groups, nx + 1, part, size), f32),
            vmem((nx, part, wide), f32),
            vmem((groups, size + part, size), f32),
            vmem((groups, part, size), f32),
            vmem((groups, part, size), f32),
            vmem((nx, part, size), f32),
            vmem((cols, size), f32),
            dma((n_vecs,)), dma((n_vecs,)), dma((nx,)), dma((nx,)),
            dma((far, groups, 2)), dma((far, groups, 2)), dma((far, groups, 2)), dma((far, groups, 2)),
            dma((groups,)), dma((groups,)), dma((groups,)), dma((groups,)), dma((nx,)), dma((nx,)),
        ],
        compiler_params=pltpu.CompilerParams(collective_id=0, has_side_effects=True),
        name="rows",
    )(vectors, reflectors)
    return out.T


def solution(mesh):
    n_rows, n_vecs = mesh.shape["rows"], mesh.shape["vecs"]
    placed = (P("rows", "vecs"), P(None, "rows", "vecs", None))
    return jax.shard_map(
        functools.partial(local, n_rows, n_vecs, ACROSS), mesh=mesh, in_specs=placed,
        out_specs=P("rows", "vecs"), check_vma=False)
```

```python
import functools

import jax
import jax.numpy as jnp
from jax import lax
from jax.experimental import pallas as pl
from jax.experimental.pallas import tpu as pltpu
from jax.sharding import PartitionSpec as P

HIGHEST = lax.Precision.HIGHEST
MESH = pl.DeviceIdType.MESH
ACROSS = 8


def hdot(a, b):
    return jnp.dot(a, b, precision=HIGHEST, preferred_element_type=jnp.float32)


def split(value):
    high = value.astype(jnp.bfloat16)
    low = (value - high.astype(jnp.float32)).astype(jnp.bfloat16)
    return high, low


def product3(left, right):
    (left_high, left_low), (right_high, right_low) = split(left), split(right)

    def dot(a, b):
        return jnp.dot(a, b, preferred_element_type=jnp.float32)

    return dot(left_high, right_high) + (dot(left_low, right_high) + dot(left_high, right_low))


def inverse_factors(blocks):
    n = blocks[0].shape[0]
    row = lax.broadcasted_iota(jnp.int32, (n, n), 0)
    col = lax.broadcasted_iota(jnp.int32, (n, n), 1)
    stricts, halves = [], []
    for block in blocks:
        gram = lax.dot_general(block, block, (((1,), (1,)), ((), ())), precision=HIGHEST,
                               preferred_element_type=jnp.float32)
        diagonal = jnp.where(row == col, gram * 0.5, 0.0)
        halves.append(jnp.sum(diagonal, axis=1, keepdims=True))
        stricts.append(jnp.where(row > col, gram / jnp.sum(diagonal, axis=0, keepdims=True), 0.0))
    identity = jnp.where(row == col, 1.0, 0.0).astype(jnp.float32)
    results = [identity] * len(blocks)
    size = 1
    while size < n:
        wide = 2 * size
        pair = (row // wide == col // wide) & (row % wide >= size) & (col % wide < size)
        corners = [jnp.where(pair, strict, 0.0) for strict in stricts]
        if size == 1:
            results = [result - corner for result, corner in zip(results, corners)]
        else:
            halfway = [product3(result, corner) for result, corner in zip(results, corners)]
            results = [result - product3(half, result) for result, half in zip(results, halfway)]
        size = wide
    return [result / half for result, half in zip(results, halves)]


def kernel(n_rows, n_vecs, nx, x_ref, refl_ref, out_ref, blocks, factors, maps, turned, state, base, skip, carry,
           passed, ready, final, ag_send, ag_recv, in_send, in_recv, ring_send, ring_recv, share_send,
           share_recv, low_send, low_recv, car_send, car_recv, fin_send, fin_recv):
    groups, size, wide = blocks.shape[1:]
    cols = x_ref.shape[1]
    part = cols // nx
    ny = n_rows // nx
    n_chips = n_vecs // 2
    piece = size // n_vecs
    r, v = lax.axis_index("rows"), lax.axis_index("vecs")
    y, x = r // nx, lax.rem(r, nx)
    core = lax.rem(v, 2)
    partner = v + 1 - 2 * core
    first, last = y == 0, y == ny - 1
    inner, outer = jnp.logical_not(first), jnp.logical_not(last)
    above = (lax.rem(r + n_rows - nx, n_rows), v)
    below = (lax.rem(r + nx, n_rows), v)
    mate = (r, partner)
    way = 1 - 2 * core

    def along(step):
        return lax.rem(x + step + 2 * nx, nx)

    def remote(src, dst, sent, got, device):
        return pltpu.make_async_remote_copy(src, dst, sent, got, device_id=device, device_id_type=MESH)

    onward = (y * nx + along(way), v)
    chips = [lax.rem(v + 2 * k, n_vecs) for k in range(1, n_chips)]
    peers = [along(k) for k in range(1, nx)]

    barrier = pltpu.get_barrier_semaphore()
    for device in [mate, above, below] + [(r, c) for c in chips] + [(y * nx + p, v) for p in peers]:
        pl.semaphore_signal(barrier, inc=1, device_id=device, device_id_type=MESH)
    pl.semaphore_wait(barrier, 3 + len(chips) + len(peers))

    def rows_of(vec):
        return pl.ds(pl.multiple_of(vec * piece, piece), piece)

    def cols_of(place):
        return pl.ds(pl.multiple_of(place * part, part), part)

    sends = []
    halves = (slice(0, 1), slice(1, groups))

    def shard(half, vec):
        return blocks.at[x, halves[half], rows_of(vec)]

    for half in range(2):
        for k, peer in enumerate(chips + [partner]):
            sends.append(remote(refl_ref.at[halves[half], 0], shard(half, v), ag_send.at[half, k], ag_recv.at[half, v], (r, peer)))
            sends[-1].start()

    turned[...] = x_ref[...].T
    for k, peer in enumerate(peers):
        sends.append(remote(turned.at[cols_of(peer)], state.at[0, x], in_send.at[k], in_recv.at[x], (y * nx + peer, v)))
        sends[-1].start()
    state[0, x] = turned[cols_of(x)]
    blocks[x, :, rows_of(v)] = refl_ref[:, 0]

    @pl.when(last)
    def _():
        for g in range(groups):
            state[g, nx] = jnp.zeros((part, size), jnp.float32)

    def arrived(half, vec):
        remote(refl_ref.at[halves[half], 0], shard(half, vec), ag_send.at[half, 0], ag_recv.at[half, vec], mate).wait_recv()

    order = sorted(range(1, n_chips), key=lambda k: min(k, n_chips - k))

    def gather(half):
        for k in order:
            source = lax.rem(v - 2 * k + n_vecs, n_vecs)
            arrived(half, source)
            there = shard(half, source)
            sends.append(remote(there, there, ag_send.at[half, n_chips + k - 1], ag_recv.at[half, source], mate))
            sends[-1].start()
        arrived(half, partner)
        for k in order:
            arrived(half, lax.rem(partner - 2 * k + n_vecs, n_vecs))

    gather(0)

    far = nx // 2
    stores = (blocks, factors)

    def ring(step, g, kind):
        there = stores[kind].at[along(-way * (step - 1)), g]
        return remote(there, there, ring_send.at[step - 1, g, kind], ring_recv.at[step - 1, g, kind], onward)

    def ring_arrival(step, g, kind):
        there = stores[kind].at[along(-way * step), g]
        return remote(there, there, ring_send.at[step - 1, g, kind], ring_recv.at[step - 1, g, kind], onward)

    def share(step, g, kind, sign):
        there = stores[kind].at[along(-sign * way * step), g]
        return remote(there, there, share_send.at[step - 1, g, kind], share_recv.at[step - 1, g, kind], mate)

    def owner(step, kind):
        return None if step < far else kind

    def on(core_index, action):
        if core_index is None:
            action()
        else:
            pl.when(core == core_index)(action)

    def launch(g, kind):
        on(owner(1, kind), lambda: ring(1, g, kind).start())

    launch(0, 0)

    def low(g):
        return remote(state.at[g, 0], state.at[g, nx], low_send.at[g], low_recv.at[g], above)

    lane = lax.broadcasted_iota(jnp.int32, (size, wide), 1)

    def masked(place, g):
        return jnp.where((y * nx + place < n_rows - 1) | (lane < size), blocks[place, g], 0.0)

    def factor(*own):
        for g, inverse in zip(own, inverse_factors([masked(x, g) for g in own])):
            factors[x, g] = inverse

    def form(place, g):
        block = masked(place, g)
        full = product3(block.T, product3(factors[place, g], block))
        maps[place, g, 0], maps[place, g, 1] = split(full)

    def spread(slot):
        here = [(slot - g, g) for g in range(groups) if 1 <= slot - g <= far]
        for step, g in here:
            for kind in range(2):
                def take():
                    ring_arrival(step, g, kind).wait_recv()
                    if step < far:
                        on(owner(step + 1, kind), lambda: ring(step + 1, g, kind).start())
                    share(step, g, kind, 1).start()

                on(owner(step, kind), take)
        if slot < groups:
            launch(slot, 0)
            if slot == 1:
                factor(*range(1, groups))
            launch(slot, 1)
            form(x, slot)
        for step, g in here:
            if step < far:
                form(along(-way * step), g)
            for kind in range(2):
                whose = owner(step, kind)
                on(None if whose is None else 1 - whose, lambda: share(step, g, kind, -1).wait_recv())
            form(along(way * step), g)

    factor(0)
    launch(0, 1)
    form(x, 0)
    gather(1)

    def product(value, place, g, half):
        at = slice(half * size, (half + 1) * size)
        high, lower = split(value)
        both = jnp.dot(jnp.concatenate([high, lower], axis=0), maps[place, g, 0, at], preferred_element_type=jnp.float32)
        cross = jnp.dot(high, maps[place, g, 1, at], preferred_element_type=jnp.float32)
        return both[:part] + (both[part:] + cross)

    def pass_on(g):
        return remote(passed.at[g], carry.at[g], car_send.at[g], car_recv.at[g], below)

    def deliver(place, slot):
        return remote(ready.at[slot], final.at[cols_of(x)], fin_send.at[slot], fin_recv.at[x], (y * nx + place, v))

    def prepare(g, place):
        under = state[g, place + 1]
        taken = product(under, place, g, 1)
        base[place, :, :size] = -taken[:, :size]
        base[place, :, size:] = under - taken[:, size:]

    def send_carry(g):
        @pl.when(outer)
        def _():
            pass_on(g).start()

    def begin(g, at_first):
        for place in range(nx - 1):
            prepare(g, place)
        if at_first:
            return
        right = slice(size, wide)
        start = maps[0, g, 0, :size, right].astype(jnp.float32) + maps[0, g, 1, :size, right].astype(jnp.float32)
        through = jnp.concatenate([-start, base[0, :, right]], axis=0)
        rows = size + part
        for place in range(1, nx):
            high, lower = split(through)
            both = jnp.dot(jnp.concatenate([high, lower], axis=0), maps[place, g, 0, :size, right],
                           preferred_element_type=jnp.float32)
            cross = jnp.dot(high, maps[place, g, 1, :size, right], preferred_element_type=jnp.float32)
            through = -(both[:rows] + (both[rows:] + cross))
            if place < nx - 1:
                through = jnp.concatenate([through[:size], through[size:] + base[place, :, right]], axis=0)
        skip[g] = through

    def chain(g, at_first):
        @pl.when(outer)
        def _():
            low(g).wait_recv()

        prepare(g, nx - 1)
        if at_first:
            top = state[g, 0]
        else:
            pass_on(g).wait_recv()
            top = carry[g]
            passed[g] = product3(top, skip[g, :size]) + (skip[g, size:] + base[nx - 1, :, size:])
            send_carry(g)
        for place in range(nx):
            result = base[place] - product(top, place, g, 0)
            done = top + result[:, :size]
            top = result[:, size:]
            if g < groups - 1:
                state[g + 1, place] = done
                if place == 0 and not at_first:
                    low(g + 1).start()
            else:
                ready[place] = done

                @pl.when(x != place)
                def _():
                    deliver(place, place).start()
        if at_first:
            passed[g] = top
            send_carry(g)

    early = inner & (y <= 2)
    spread(1)
    for k in range(1, nx):
        source = along(-k)
        remote(turned.at[cols_of(x)], state.at[0, source], in_send.at[0], in_recv.at[source], onward).wait_recv()

    @pl.when(inner)
    def _():
        low(0).start()

    for slot in range(2, far + 1):
        spread(slot)

    @pl.when(first)
    def _():
        begin(0, True)
        chain(0, True)

    @pl.when(inner)
    def _():
        begin(0, False)

    spread(far + 1)

    @pl.when(first)
    def _():
        begin(1, True)
        chain(1, True)

    @pl.when(early)
    def _():
        chain(0, False)
        begin(1, False)

    for slot in range(far + 2, far + groups):
        spread(slot)

    @pl.when(y > 2)
    def _():
        chain(0, False)
        begin(1, False)

    @pl.when(inner)
    def _():
        chain(1, False)

    for at_first, condition in ((True, first), (False, inner)):
        @pl.when(condition)
        def _():
            for g in range(2, groups):
                begin(g, at_first)
                chain(g, at_first)

    final[cols_of(x)] = ready[x]
    for k in range(1, nx):
        source = along(-k)
        remote(ready.at[0], final.at[cols_of(source)], fin_send.at[0], fin_recv.at[source], onward).wait_recv()
    out_ref[...] = final[...]

    for copy in sends:
        copy.wait_send()
    for step in range(1, far + 1):
        for kind in range(2):
            for g in range(groups):
                def finish():
                    ring(step, g, kind).wait_send()
                    share(step, g, kind, 1).wait_send()

                on(owner(step, kind), finish)
    for place in range(nx):
        @pl.when(x != place)
        def _():
            deliver(place, place).wait_send()

    @pl.when(outer)
    def _():
        for g in range(groups):
            pass_on(g).wait_send()

    @pl.when(inner)
    def _():
        for g in range(groups):
            low(g).wait_send()


def local(n_rows, n_vecs, nx, vectors, reflectors):
    size, cols = vectors.shape
    groups, wide = reflectors.shape[0], reflectors.shape[3]
    part, far, f32, vmem = cols // nx, nx // 2, jnp.float32, pltpu.VMEM
    dma = pltpu.SemaphoreType.DMA
    out = pl.pallas_call(
        functools.partial(kernel, n_rows, n_vecs, nx),
        out_shape=jax.ShapeDtypeStruct((cols, size), f32),
        in_specs=[pl.BlockSpec(memory_space=vmem)] * 2,
        out_specs=pl.BlockSpec(memory_space=vmem),
        scratch_shapes=[
            vmem((nx, groups, size, wide), f32),
            vmem((nx, groups, size, size), f32),
            vmem((nx, groups, 2, wide, wide), jnp.bfloat16),
            vmem((cols, size), f32),
            vmem((groups, nx + 1, part, size), f32),
            vmem((nx, part, wide), f32),
            vmem((groups, size + part, size), f32),
            vmem((groups, part, size), f32),
            vmem((groups, part, size), f32),
            vmem((nx, part, size), f32),
            vmem((cols, size), f32),
            dma((2, n_vecs)), dma((2, n_vecs)), dma((nx,)), dma((nx,)),
            dma((far, groups, 2)), dma((far, groups, 2)), dma((far, groups, 2)), dma((far, groups, 2)),
            dma((groups,)), dma((groups,)), dma((groups,)), dma((groups,)), dma((nx,)), dma((nx,)),
        ],
        compiler_params=pltpu.CompilerParams(collective_id=0, has_side_effects=True),
        name="rows",
    )(vectors, reflectors)
    return out.T


def solution(mesh):
    n_rows, n_vecs = mesh.shape["rows"], mesh.shape["vecs"]
    placed = (P("rows", "vecs"), P(None, "rows", "vecs", None))
    return jax.shard_map(
        functools.partial(local, n_rows, n_vecs, ACROSS), mesh=mesh, in_specs=placed,
        out_specs=P("rows", "vecs"), check_vma=False)
```

```python
import functools

import jax
import jax.numpy as jnp
from jax import lax
from jax.experimental import pallas as pl
from jax.experimental.pallas import tpu as pltpu
from jax.sharding import PartitionSpec as P

HIGHEST = lax.Precision.HIGHEST
MESH = pl.DeviceIdType.MESH
ACROSS = 8


def hdot(a, b):
    return jnp.dot(a, b, precision=HIGHEST, preferred_element_type=jnp.float32)


def split(value):
    high = value.astype(jnp.bfloat16)
    low = (value - high.astype(jnp.float32)).astype(jnp.bfloat16)
    return high, low


def product3(left, right):
    (left_high, left_low), (right_high, right_low) = split(left), split(right)

    def dot(a, b):
        return jnp.dot(a, b, preferred_element_type=jnp.float32)

    return dot(left_high, right_high) + (dot(left_low, right_high) + dot(left_high, right_low))


def inverse_factors(blocks):
    n = blocks[0].shape[0]
    row = lax.broadcasted_iota(jnp.int32, (n, n), 0)
    col = lax.broadcasted_iota(jnp.int32, (n, n), 1)
    stricts, halves = [], []
    for block in blocks:
        gram = lax.dot_general(block, block, (((1,), (1,)), ((), ())), precision=HIGHEST,
                               preferred_element_type=jnp.float32)
        diagonal = jnp.where(row == col, gram * 0.5, 0.0)
        halves.append(jnp.sum(diagonal, axis=1, keepdims=True))
        stricts.append(jnp.where(row > col, gram / jnp.sum(diagonal, axis=0, keepdims=True), 0.0))
    identity = jnp.where(row == col, 1.0, 0.0).astype(jnp.float32)
    results = [identity] * len(blocks)
    size = 1
    while size < n:
        wide = 2 * size
        pair = (row // wide == col // wide) & (row % wide >= size) & (col % wide < size)
        corners = [jnp.where(pair, strict, 0.0) for strict in stricts]
        if size == 1:
            results = [result - corner for result, corner in zip(results, corners)]
        else:
            halfway = [product3(result, corner) for result, corner in zip(results, corners)]
            results = [result - product3(half, result) for result, half in zip(results, halfway)]
        size = wide
    return [result / half for result, half in zip(results, halves)]


def kernel(n_rows, n_vecs, nx, x_ref, refl_ref, out_ref, blocks, factors, maps, turned, state, base, skip, alone, carry,
           passed, ready, final, ag_send, ag_recv, in_send, in_recv, ring_send, ring_recv, share_send,
           share_recv, low_send, low_recv, car_send, car_recv, fin_send, fin_recv):
    groups, size, wide = blocks.shape[1:]
    cols = x_ref.shape[1]
    part = cols // nx
    ny = n_rows // nx
    n_chips = n_vecs // 2
    piece = size // n_vecs
    r, v = lax.axis_index("rows"), lax.axis_index("vecs")
    y, x = r // nx, lax.rem(r, nx)
    core = lax.rem(v, 2)
    partner = v + 1 - 2 * core
    first, last = y == 0, y == ny - 1
    inner, outer = jnp.logical_not(first), jnp.logical_not(last)
    above = (lax.rem(r + n_rows - nx, n_rows), v)
    below = (lax.rem(r + nx, n_rows), v)
    mate = (r, partner)
    way = 1 - 2 * core

    def along(step):
        return lax.rem(x + step + 2 * nx, nx)

    def remote(src, dst, sent, got, device):
        return pltpu.make_async_remote_copy(src, dst, sent, got, device_id=device, device_id_type=MESH)

    onward = (y * nx + along(way), v)
    chips = [lax.rem(v + 2 * k, n_vecs) for k in range(1, n_chips)]
    peers = [along(k) for k in range(1, nx)]

    barrier = pltpu.get_barrier_semaphore()
    for device in [mate, above, below] + [(r, c) for c in chips] + [(y * nx + p, v) for p in peers]:
        pl.semaphore_signal(barrier, inc=1, device_id=device, device_id_type=MESH)
    pl.semaphore_wait(barrier, 3 + len(chips) + len(peers))

    def rows_of(vec):
        return pl.ds(pl.multiple_of(vec * piece, piece), piece)

    def cols_of(place):
        return pl.ds(pl.multiple_of(place * part, part), part)

    sends = []
    halves = (slice(0, 1), slice(1, groups))

    def shard(half, vec):
        return blocks.at[x, halves[half], rows_of(vec)]

    for half in range(2):
        for k, peer in enumerate(chips + [partner]):
            sends.append(remote(refl_ref.at[halves[half], 0], shard(half, v), ag_send.at[half, k], ag_recv.at[half, v], (r, peer)))
            sends[-1].start()

    turned[...] = x_ref[...].T
    for k, peer in enumerate(peers):
        sends.append(remote(turned.at[cols_of(peer)], state.at[0, x], in_send.at[k], in_recv.at[x], (y * nx + peer, v)))
        sends[-1].start()
    state[0, x] = turned[cols_of(x)]
    blocks[x, :, rows_of(v)] = refl_ref[:, 0]

    @pl.when(last)
    def _():
        for g in range(groups):
            state[g, nx] = jnp.zeros((part, size), jnp.float32)

    def arrived(half, vec):
        remote(refl_ref.at[halves[half], 0], shard(half, vec), ag_send.at[half, 0], ag_recv.at[half, vec], mate).wait_recv()

    order = sorted(range(1, n_chips), key=lambda k: min(k, n_chips - k))

    def gather(half):
        for k in order:
            source = lax.rem(v - 2 * k + n_vecs, n_vecs)
            arrived(half, source)
            there = shard(half, source)
            sends.append(remote(there, there, ag_send.at[half, n_chips + k - 1], ag_recv.at[half, source], mate))
            sends[-1].start()
        arrived(half, partner)
        for k in order:
            arrived(half, lax.rem(partner - 2 * k + n_vecs, n_vecs))

    gather(0)

    far = nx // 2
    stores = (blocks, factors)

    def ring(step, g, kind):
        there = stores[kind].at[along(-way * (step - 1)), g]
        return remote(there, there, ring_send.at[step - 1, g, kind], ring_recv.at[step - 1, g, kind], onward)

    def ring_arrival(step, g, kind):
        there = stores[kind].at[along(-way * step), g]
        return remote(there, there, ring_send.at[step - 1, g, kind], ring_recv.at[step - 1, g, kind], onward)

    def share(step, g, kind, sign):
        there = stores[kind].at[along(-sign * way * step), g]
        return remote(there, there, share_send.at[step - 1, g, kind], share_recv.at[step - 1, g, kind], mate)

    def launch(g, kind):
        ring(1, g, kind).start()

    launch(0, 0)

    def low(g):
        return remote(state.at[g, 0], state.at[g, nx], low_send.at[g], low_recv.at[g], above)

    lane = lax.broadcasted_iota(jnp.int32, (size, wide), 1)

    def masked(place, g):
        return jnp.where((y * nx + place < n_rows - 1) | (lane < size), blocks[place, g], 0.0)

    def factor(*own):
        for g, inverse in zip(own, inverse_factors([masked(x, g) for g in own])):
            factors[x, g] = inverse

    def form(place, g):
        block = masked(place, g)
        full = product3(block.T, product3(factors[place, g], block))
        maps[place, g, 0], maps[place, g, 1] = split(full)

    def spread(slot):
        here = [(slot - g, g) for g in range(groups) if 1 <= slot - g <= far]
        for step, g in here:
            for kind in range(2):
                ring_arrival(step, g, kind).wait_recv()
                if step < far:
                    ring(step + 1, g, kind).start()
                    share(step, g, kind, 1).start()
        if slot < groups:
            launch(slot, 0)
            if slot == 1:
                factor(*range(1, groups))
            launch(slot, 1)
            form(x, slot)
        for step, g in here:
            form(along(-way * step), g)
            if step < far:
                for kind in range(2):
                    share(step, g, kind, -1).wait_recv()
                form(along(way * step), g)

    factor(0)
    launch(0, 1)
    form(x, 0)
    gather(1)

    def product(value, place, g, half):
        at = slice(half * size, (half + 1) * size)
        high, lower = split(value)
        both = jnp.dot(jnp.concatenate([high, lower], axis=0), maps[place, g, 0, at], preferred_element_type=jnp.float32)
        cross = jnp.dot(high, maps[place, g, 1, at], preferred_element_type=jnp.float32)
        return both[:part] + (both[part:] + cross)

    def pass_on(g):
        return remote(passed.at[g], carry.at[g], car_send.at[g], car_recv.at[g], below)

    def deliver(place, slot):
        return remote(ready.at[slot], final.at[cols_of(x)], fin_send.at[slot], fin_recv.at[x], (y * nx + place, v))

    def prepare(g, place):
        under = state[g, place + 1]
        taken = product(under, place, g, 1)
        base[place, :, :size] = -taken[:, :size]
        base[place, :, size:] = under - taken[:, size:]

    def send_carry(g):
        @pl.when(outer)
        def _():
            pass_on(g).start()

    def begin(g, at_first):
        for place in range(nx - 1):
            prepare(g, place)
        if at_first:
            return
        right = slice(size, wide)
        start = maps[0, g, 0, :size, right].astype(jnp.float32) + maps[0, g, 1, :size, right].astype(jnp.float32)
        through = jnp.concatenate([-start, base[0, :, right]], axis=0)
        rows = size + part
        for place in range(1, nx):
            high, lower = split(through)
            both = jnp.dot(jnp.concatenate([high, lower], axis=0), maps[place, g, 0, :size, right],
                           preferred_element_type=jnp.float32)
            cross = jnp.dot(high, maps[place, g, 1, :size, right], preferred_element_type=jnp.float32)
            through = -(both[:rows] + (both[rows:] + cross))
            if place < nx - 1:
                through = jnp.concatenate([through[:size], through[size:] + base[place, :, right]], axis=0)
        skip[g, 0], skip[g, 1] = split(through[:size])
        alone[g] = through[size:]

    def chain(g, at_first):
        @pl.when(outer)
        def _():
            low(g).wait_recv()

        prepare(g, nx - 1)
        if at_first:
            top = state[g, 0]
        else:
            pass_on(g).wait_recv()
            top = carry[g]
            high, lower = split(top)
            both = jnp.dot(jnp.concatenate([high, lower], axis=0), skip[g, 0], preferred_element_type=jnp.float32)
            cross = jnp.dot(high, skip[g, 1], preferred_element_type=jnp.float32)
            passed[g] = both[:part] + (both[part:] + cross) + (alone[g] + base[nx - 1, :, size:])
            send_carry(g)
        for place in range(nx):
            result = base[place] - product(top, place, g, 0)
            done = top + result[:, :size]
            top = result[:, size:]
            if g < groups - 1:
                state[g + 1, place] = done
                if place == 0 and not at_first:
                    low(g + 1).start()
            else:
                ready[place] = done

                @pl.when(x != place)
                def _():
                    deliver(place, place).start()
        if at_first:
            passed[g] = top
            send_carry(g)

    spread(1)
    for k in range(1, nx):
        source = along(-k)
        remote(turned.at[cols_of(x)], state.at[0, source], in_send.at[0], in_recv.at[source], onward).wait_recv()

    @pl.when(inner)
    def _():
        low(0).start()

    for slot in range(2, far + 1):
        spread(slot)

    @pl.when(first)
    def _():
        begin(0, True)
        chain(0, True)

    @pl.when(inner)
    def _():
        begin(0, False)

    @pl.when(y == 1)
    def _():
        chain(0, False)

    spread(far + 1)

    @pl.when(first)
    def _():
        begin(1, True)
        chain(1, True)

    @pl.when(y == 2)
    def _():
        chain(0, False)

    @pl.when(inner & (y <= 2))
    def _():
        begin(1, False)

    for slot in range(far + 2, far + groups):
        spread(slot)

    @pl.when(y > 2)
    def _():
        chain(0, False)
        begin(1, False)

    @pl.when(inner)
    def _():
        chain(1, False)

    for at_first, condition in ((True, first), (False, inner)):
        @pl.when(condition)
        def _():
            for g in range(2, groups):
                begin(g, at_first)
                chain(g, at_first)

    final[cols_of(x)] = ready[x]
    for k in range(1, nx):
        source = along(-k)
        remote(ready.at[0], final.at[cols_of(source)], fin_send.at[0], fin_recv.at[source], onward).wait_recv()
    out_ref[...] = final[...]

    for copy in sends:
        copy.wait_send()
    for step in range(1, far + 1):
        for kind in range(2):
            for g in range(groups):
                ring(step, g, kind).wait_send()
                if step < far:
                    share(step, g, kind, 1).wait_send()
    for place in range(nx):
        @pl.when(x != place)
        def _():
            deliver(place, place).wait_send()

    @pl.when(outer)
    def _():
        for g in range(groups):
            pass_on(g).wait_send()

    @pl.when(inner)
    def _():
        for g in range(groups):
            low(g).wait_send()


def local(n_rows, n_vecs, nx, vectors, reflectors):
    size, cols = vectors.shape
    groups, wide = reflectors.shape[0], reflectors.shape[3]
    part, far, f32, vmem = cols // nx, nx // 2, jnp.float32, pltpu.VMEM
    dma = pltpu.SemaphoreType.DMA
    out = pl.pallas_call(
        functools.partial(kernel, n_rows, n_vecs, nx),
        out_shape=jax.ShapeDtypeStruct((cols, size), f32),
        in_specs=[pl.BlockSpec(memory_space=vmem)] * 2,
        out_specs=pl.BlockSpec(memory_space=vmem),
        scratch_shapes=[
            vmem((nx, groups, size, wide), f32),
            vmem((nx, groups, size, size), f32),
            vmem((nx, groups, 2, wide, wide), jnp.bfloat16),
            vmem((cols, size), f32),
            vmem((groups, nx + 1, part, size), f32),
            vmem((nx, part, wide), f32),
            vmem((groups, 2, size, size), jnp.bfloat16),
            vmem((groups, part, size), f32),
            vmem((groups, part, size), f32),
            vmem((groups, part, size), f32),
            vmem((nx, part, size), f32),
            vmem((cols, size), f32),
            dma((2, n_vecs)), dma((2, n_vecs)), dma((nx,)), dma((nx,)),
            dma((far, groups, 2)), dma((far, groups, 2)), dma((far, groups, 2)), dma((far, groups, 2)),
            dma((groups,)), dma((groups,)), dma((groups,)), dma((groups,)), dma((nx,)), dma((nx,)),
        ],
        compiler_params=pltpu.CompilerParams(collective_id=0, has_side_effects=True),
        name="rows",
    )(vectors, reflectors)
    return out.T


def solution(mesh):
    n_rows, n_vecs = mesh.shape["rows"], mesh.shape["vecs"]
    placed = (P("rows", "vecs"), P(None, "rows", "vecs", None))
    return jax.shard_map(
        functools.partial(local, n_rows, n_vecs, ACROSS), mesh=mesh, in_specs=placed,
        out_specs=P("rows", "vecs"), check_vma=False)
```

```python
import functools

import jax
import jax.numpy as jnp
from jax import lax
from jax.experimental import pallas as pl
from jax.experimental.pallas import tpu as pltpu
from jax.sharding import PartitionSpec as P

HIGHEST = lax.Precision.HIGHEST
MESH = pl.DeviceIdType.MESH
ACROSS = 8


def hdot(a, b):
    return jnp.dot(a, b, precision=HIGHEST, preferred_element_type=jnp.float32)


def split(value):
    high = value.astype(jnp.bfloat16)
    low = (value - high.astype(jnp.float32)).astype(jnp.bfloat16)
    return high, low


def product3(left, right):
    (left_high, left_low), (right_high, right_low) = split(left), split(right)

    def dot(a, b):
        return jnp.dot(a, b, preferred_element_type=jnp.float32)

    return dot(left_high, right_high) + (dot(left_low, right_high) + dot(left_high, right_low))


def inverse_factors(blocks):
    n = blocks[0].shape[0]
    row = lax.broadcasted_iota(jnp.int32, (n, n), 0)
    col = lax.broadcasted_iota(jnp.int32, (n, n), 1)
    stricts, halves = [], []
    for block in blocks:
        gram = lax.dot_general(block, block, (((1,), (1,)), ((), ())), precision=HIGHEST,
                               preferred_element_type=jnp.float32)
        diagonal = jnp.where(row == col, gram * 0.5, 0.0)
        halves.append(jnp.sum(diagonal, axis=1, keepdims=True))
        stricts.append(jnp.where(row > col, gram / jnp.sum(diagonal, axis=0, keepdims=True), 0.0))
    identity = jnp.where(row == col, 1.0, 0.0).astype(jnp.float32)
    results = [identity] * len(blocks)
    size = 1
    while size < n:
        wide = 2 * size
        pair = (row // wide == col // wide) & (row % wide >= size) & (col % wide < size)
        corners = [jnp.where(pair, strict, 0.0) for strict in stricts]
        if size == 1:
            results = [result - corner for result, corner in zip(results, corners)]
        else:
            halfway = [product3(result, corner) for result, corner in zip(results, corners)]
            results = [result - product3(half, result) for result, half in zip(results, halfway)]
        size = wide
    return [result / half for result, half in zip(results, halves)]


def kernel(n_rows, n_vecs, nx, x_ref, refl_ref, out_ref, blocks, factors, maps, turned, state, base, skip, alone, carry,
           passed, ready, final, ag_send, ag_recv, in_send, in_recv, ring_send, ring_recv, share_send,
           share_recv, low_send, low_recv, car_send, car_recv, fin_send, fin_recv):
    groups, size, wide = blocks.shape[1:]
    cols = x_ref.shape[1]
    part = cols // nx
    ny = n_rows // nx
    n_chips = n_vecs // 2
    piece = size // n_vecs
    r, v = lax.axis_index("rows"), lax.axis_index("vecs")
    y, x = r // nx, lax.rem(r, nx)
    core = lax.rem(v, 2)
    partner = v + 1 - 2 * core
    first, last = y == 0, y == ny - 1
    inner, outer = jnp.logical_not(first), jnp.logical_not(last)
    above = (lax.rem(r + n_rows - nx, n_rows), v)
    below = (lax.rem(r + nx, n_rows), v)
    mate = (r, partner)
    way = 1 - 2 * core

    def along(step):
        return lax.rem(x + step + 2 * nx, nx)

    def remote(src, dst, sent, got, device):
        return pltpu.make_async_remote_copy(src, dst, sent, got, device_id=device, device_id_type=MESH)

    onward = (y * nx + along(way), v)
    chips = [lax.rem(v + 2 * k, n_vecs) for k in range(1, n_chips)]
    peers = [along(k) for k in range(1, nx)]

    barrier = pltpu.get_barrier_semaphore()
    for device in [mate, above, below] + [(r, c) for c in chips] + [(y * nx + p, v) for p in peers]:
        pl.semaphore_signal(barrier, inc=1, device_id=device, device_id_type=MESH)
    pl.semaphore_wait(barrier, 3 + len(chips) + len(peers))

    def rows_of(vec):
        return pl.ds(pl.multiple_of(vec * piece, piece), piece)

    def cols_of(place):
        return pl.ds(pl.multiple_of(place * part, part), part)

    sends = []
    halves = (slice(0, 1), slice(1, groups))

    def shard(half, vec):
        return blocks.at[x, halves[half], rows_of(vec)]

    for half in range(2):
        for k, peer in enumerate(chips + [partner]):
            sends.append(remote(refl_ref.at[halves[half], 0], shard(half, v), ag_send.at[half, k], ag_recv.at[half, v], (r, peer)))
            sends[-1].start()

    turned[...] = x_ref[...].T
    for k, peer in enumerate(peers):
        sends.append(remote(turned.at[cols_of(peer)], state.at[0, x], in_send.at[k], in_recv.at[x], (y * nx + peer, v)))
        sends[-1].start()
    state[0, x] = turned[cols_of(x)]
    blocks[x, :, rows_of(v)] = refl_ref[:, 0]

    @pl.when(last)
    def _():
        for g in range(groups):
            state[g, nx] = jnp.zeros((part, size), jnp.float32)

    def arrived(half, vec):
        remote(refl_ref.at[halves[half], 0], shard(half, vec), ag_send.at[half, 0], ag_recv.at[half, vec], mate).wait_recv()

    order = sorted(range(1, n_chips), key=lambda k: min(k, n_chips - k))

    def gather(half):
        for k in order:
            source = lax.rem(v - 2 * k + n_vecs, n_vecs)
            arrived(half, source)
            there = shard(half, source)
            sends.append(remote(there, there, ag_send.at[half, n_chips + k - 1], ag_recv.at[half, source], mate))
            sends[-1].start()
        arrived(half, partner)
        for k in order:
            arrived(half, lax.rem(partner - 2 * k + n_vecs, n_vecs))

    gather(0)

    far = nx // 2
    stores = (blocks, factors)

    def ring(step, g, kind):
        there = stores[kind].at[along(-way * (step - 1)), g]
        return remote(there, there, ring_send.at[step - 1, g, kind], ring_recv.at[step - 1, g, kind], onward)

    def ring_arrival(step, g, kind):
        there = stores[kind].at[along(-way * step), g]
        return remote(there, there, ring_send.at[step - 1, g, kind], ring_recv.at[step - 1, g, kind], onward)

    def share(step, g, kind, sign):
        there = stores[kind].at[along(-sign * way * step), g]
        return remote(there, there, share_send.at[step - 1, g, kind], share_recv.at[step - 1, g, kind], mate)

    def owner(step, kind):
        return None if step < far else kind

    def on(core_index, action):
        if core_index is None:
            action()
        else:
            pl.when(core == core_index)(action)

    def launch(g, kind):
        on(owner(1, kind), lambda: ring(1, g, kind).start())

    launch(0, 0)

    def low(g):
        return remote(state.at[g, 0], state.at[g, nx], low_send.at[g], low_recv.at[g], above)

    lane = lax.broadcasted_iota(jnp.int32, (size, wide), 1)

    def masked(place, g):
        return jnp.where((y * nx + place < n_rows - 1) | (lane < size), blocks[place, g], 0.0)

    def factor(*own):
        for g, inverse in zip(own, inverse_factors([masked(x, g) for g in own])):
            factors[x, g] = inverse

    def form(place, g):
        block = masked(place, g)
        full = product3(block.T, product3(factors[place, g], block))
        maps[place, g, 0], maps[place, g, 1] = split(full)

    def spread(slot):
        here = [(slot - g, g) for g in range(groups) if 1 <= slot - g <= far]
        for step, g in here:
            for kind in range(2):
                def take():
                    ring_arrival(step, g, kind).wait_recv()
                    if step < far:
                        on(owner(step + 1, kind), lambda: ring(step + 1, g, kind).start())
                    share(step, g, kind, 1).start()

                on(owner(step, kind), take)
        if slot < groups:
            launch(slot, 0)
            if slot == 1:
                factor(*range(1, groups))
            launch(slot, 1)
            form(x, slot)
        for step, g in here:
            if step < far:
                form(along(-way * step), g)
            for kind in range(2):
                whose = owner(step, kind)
                on(None if whose is None else 1 - whose, lambda: share(step, g, kind, -1).wait_recv())
            form(along(way * step), g)

    factor(0)
    launch(0, 1)
    form(x, 0)
    gather(1)

    def product(value, place, g, half):
        at = slice(half * size, (half + 1) * size)
        high, lower = split(value)
        both = jnp.dot(jnp.concatenate([high, lower], axis=0), maps[place, g, 0, at], preferred_element_type=jnp.float32)
        cross = jnp.dot(high, maps[place, g, 1, at], preferred_element_type=jnp.float32)
        return both[:part] + (both[part:] + cross)

    def pass_on(g):
        return remote(passed.at[g], carry.at[g], car_send.at[g], car_recv.at[g], below)

    def deliver(place, slot):
        return remote(ready.at[slot], final.at[cols_of(x)], fin_send.at[slot], fin_recv.at[x], (y * nx + place, v))

    def prepare(g, place):
        under = state[g, place + 1]
        taken = product(under, place, g, 1)
        base[place, :, :size] = -taken[:, :size]
        base[place, :, size:] = under - taken[:, size:]

    def send_carry(g):
        @pl.when(outer)
        def _():
            pass_on(g).start()

    def begin(g, at_first):
        for place in range(nx - 1):
            prepare(g, place)
        if at_first:
            return
        right = slice(size, wide)
        start = maps[0, g, 0, :size, right].astype(jnp.float32) + maps[0, g, 1, :size, right].astype(jnp.float32)
        through = jnp.concatenate([-start, base[0, :, right]], axis=0)
        rows = size + part
        for place in range(1, nx):
            high, lower = split(through)
            both = jnp.dot(jnp.concatenate([high, lower], axis=0), maps[place, g, 0, :size, right],
                           preferred_element_type=jnp.float32)
            cross = jnp.dot(high, maps[place, g, 1, :size, right], preferred_element_type=jnp.float32)
            through = -(both[:rows] + (both[rows:] + cross))
            if place < nx - 1:
                through = jnp.concatenate([through[:size], through[size:] + base[place, :, right]], axis=0)
        skip[g, 0], skip[g, 1] = split(through[:size])
        alone[g] = through[size:]

    def chain(g, at_first):
        @pl.when(outer)
        def _():
            low(g).wait_recv()

        prepare(g, nx - 1)
        if at_first:
            top = state[g, 0]
        else:
            pass_on(g).wait_recv()
            top = carry[g]
            high, lower = split(top)
            both = jnp.dot(jnp.concatenate([high, lower], axis=0), skip[g, 0], preferred_element_type=jnp.float32)
            cross = jnp.dot(high, skip[g, 1], preferred_element_type=jnp.float32)
            passed[g] = both[:part] + (both[part:] + cross) + (alone[g] + base[nx - 1, :, size:])
            send_carry(g)
        for place in range(nx):
            result = base[place] - product(top, place, g, 0)
            done = top + result[:, :size]
            top = result[:, size:]
            if g < groups - 1:
                state[g + 1, place] = done
                if place == 0 and not at_first:
                    low(g + 1).start()
            else:
                ready[place] = done

                @pl.when(x != place)
                def _():
                    deliver(place, place).start()
        if at_first:
            passed[g] = top
            send_carry(g)

    spread(1)
    for k in range(1, nx):
        source = along(-k)
        remote(turned.at[cols_of(x)], state.at[0, source], in_send.at[0], in_recv.at[source], onward).wait_recv()

    @pl.when(inner)
    def _():
        low(0).start()

    for slot in range(2, far + 1):
        spread(slot)

    @pl.when(first)
    def _():
        begin(0, True)
        chain(0, True)

    @pl.when(inner)
    def _():
        begin(0, False)

    @pl.when(y == 1)
    def _():
        chain(0, False)

    spread(far + 1)

    @pl.when(first)
    def _():
        begin(1, True)
        chain(1, True)

    @pl.when(y == 2)
    def _():
        chain(0, False)

    @pl.when(inner & (y <= 2))
    def _():
        begin(1, False)

    for slot in range(far + 2, far + groups):
        spread(slot)

    @pl.when(y > 2)
    def _():
        chain(0, False)
        begin(1, False)

    @pl.when(inner)
    def _():
        chain(1, False)

    for at_first, condition in ((True, first), (False, inner)):
        @pl.when(condition)
        def _():
            for g in range(2, groups):
                begin(g, at_first)
                chain(g, at_first)

    final[cols_of(x)] = ready[x]
    for k in range(1, nx):
        source = along(-k)
        remote(ready.at[0], final.at[cols_of(source)], fin_send.at[0], fin_recv.at[source], onward).wait_recv()
    out_ref[...] = final[...]

    for copy in sends:
        copy.wait_send()
    for step in range(1, far + 1):
        for kind in range(2):
            for g in range(groups):
                def finish():
                    ring(step, g, kind).wait_send()
                    share(step, g, kind, 1).wait_send()

                on(owner(step, kind), finish)
    for place in range(nx):
        @pl.when(x != place)
        def _():
            deliver(place, place).wait_send()

    @pl.when(outer)
    def _():
        for g in range(groups):
            pass_on(g).wait_send()

    @pl.when(inner)
    def _():
        for g in range(groups):
            low(g).wait_send()


def local(n_rows, n_vecs, nx, vectors, reflectors):
    size, cols = vectors.shape
    groups, wide = reflectors.shape[0], reflectors.shape[3]
    part, far, f32, vmem = cols // nx, nx // 2, jnp.float32, pltpu.VMEM
    dma = pltpu.SemaphoreType.DMA
    out = pl.pallas_call(
        functools.partial(kernel, n_rows, n_vecs, nx),
        out_shape=jax.ShapeDtypeStruct((cols, size), f32),
        in_specs=[pl.BlockSpec(memory_space=vmem)] * 2,
        out_specs=pl.BlockSpec(memory_space=vmem),
        scratch_shapes=[
            vmem((nx, groups, size, wide), f32),
            vmem((nx, groups, size, size), f32),
            vmem((nx, groups, 2, wide, wide), jnp.bfloat16),
            vmem((cols, size), f32),
            vmem((groups, nx + 1, part, size), f32),
            vmem((nx, part, wide), f32),
            vmem((groups, 2, size, size), jnp.bfloat16),
            vmem((groups, part, size), f32),
            vmem((groups, part, size), f32),
            vmem((groups, part, size), f32),
            vmem((nx, part, size), f32),
            vmem((cols, size), f32),
            dma((2, n_vecs)), dma((2, n_vecs)), dma((nx,)), dma((nx,)),
            dma((far, groups, 2)), dma((far, groups, 2)), dma((far, groups, 2)), dma((far, groups, 2)),
            dma((groups,)), dma((groups,)), dma((groups,)), dma((groups,)), dma((nx,)), dma((nx,)),
        ],
        compiler_params=pltpu.CompilerParams(collective_id=0, has_side_effects=True),
        name="rows",
    )(vectors, reflectors)
    return out.T


def solution(mesh):
    n_rows, n_vecs = mesh.shape["rows"], mesh.shape["vecs"]
    placed = (P("rows", "vecs"), P(None, "rows", "vecs", None))
    return jax.shard_map(
        functools.partial(local, n_rows, n_vecs, ACROSS), mesh=mesh, in_specs=placed,
        out_specs=P("rows", "vecs"), check_vma=False)
```
